32 devices in a mesh: groups: 2 (over y), wide: 4 (over x, core), narrow: 4 (over z).
Axes of the slice: x: 2, y: 2, z: 4, core: 2. Of those that a mesh axis runs over, the one named last changes fastest.
Arguments:
- basis: bfloat16 [128, 64, 2, 512], P(('groups', 'wide'), 'narrow'), parts along dimension 0, may hold values from -0.25 to 0.25
- kappa: float32 [128, 64, 2], P(('groups', 'wide'), 'narrow'), parts along dimension 0, may hold values from 0.1 to 1
- velocity: float32 [3, 512], P(None, 'groups'), parts along dimension 1, may hold values from -2 to 2
- coefficients: float32 [512, 512], P('groups'), parts along dimension 0, may hold values from -6 to 6
- propagator: float32 [1024, 512], P('groups'), parts along dimension 0, may hold values from -0.25 to 0.25
Outputs:
- advanced: float32 [512, 512], P(('groups', 'wide', 'narrow')), parts along dimension 0
The draws below stay inside these ranges and needn't reach their ends.
There are 2 independent parts, one for each index of `groups`. The reference program is written for one: setup_inputs(seed, part) draws one part's arguments, and reference() takes and returns one part's arrays. A program takes and returns all parts, laid end to end along the dimension named above; each array names one. Nothing has to cross between parts.
All inputs are finite; a program needn't handle non-finite values.
Results may differ from the reference program's by a relative error of at most 0.0056.
Values may be sent and summed in bfloat16 or wider, within the bound.
No kernel may reach another device: no remote copies, remote signals or barrier semaphores. Data moves between devices by JAX's collectives and lax.ppermute only.
A program may use at most 64 MiB of HBM per device.

```python
import math
import jax
import jax.numpy as jnp
from jax import lax

R = 512
P_SIZE = 256
CX = 16
ITERS = 2
NX = 64
NY = 64
NZ = 2
N_WIDE = 4


def block_scale(rng, dims, cuts, smallest, top_value):
    factor_of, own = 1.0, jax.random.fold_in(rng, 6)
    for position, shards_of in cuts:
        draws = jnp.exp(jax.random.uniform(jax.random.fold_in(own, position), (shards_of,), jnp.float32, smallest / len(cuts), top_value / len(cuts)))
        factor_of = factor_of * jnp.repeat(draws, dims[position] // shards_of).reshape([-1 if axis == position else 1 for axis in range(len(dims))])
    return factor_of


def noise(rng, extent, deviation, bound, cuts=(), kind=jnp.bfloat16):
    values = jax.random.normal(rng, extent, jnp.float32) * deviation
    if len(cuts) > 0:
        values = block_scale(rng, extent, cuts, -0.22, 0.18) * values
    return jnp.clip(values, min=-bound, max=bound).astype(kind)


def setup_inputs(seed: int = 0, part: int = 0) -> dict:
    keys = jax.random.split(jax.random.key(seed), 6)
    part_splits = jax.random.split(jax.random.fold_in(keys[5], part), 6)
    return {
        "basis": noise(part_splits[0], (NX, NY, NZ, R), R ** -0.5, 0.25, ((0, 4), (1, 4))),
        "kappa": jnp.clip(jnp.exp(math.log(1.0) - 2.3025851 * jax.random.uniform(part_splits[1], (NX, NY, NZ), jnp.float32) ** block_scale(part_splits[1], (NX, NY, NZ), ((0, 4), (1, 4)), -0.2, 0.2)), 0.1, 1.0),
        "velocity": jnp.clip(jax.random.uniform(part_splits[2], (3, P_SIZE), jnp.float32, -2.0, 2.0), -2.0, 2.0),
        "coefficients": noise(part_splits[3], (P_SIZE, R), 1.0, 6.0, (), jnp.float32),
        "propagator": noise(part_splits[4], (R, R), R ** -0.5, 0.25, (), jnp.float32),
    }


step_size = 4.0

def forcing_of(padded, kappa, velocity):
    center = padded[1:-1, 1:-1, 1:-1].astype(jnp.float32)
    x_next = padded[2:, 1:-1, 1:-1].astype(jnp.float32)
    x_prev = padded[:-2, 1:-1, 1:-1].astype(jnp.float32)
    y_next = padded[1:-1, 2:, 1:-1].astype(jnp.float32)
    y_prev = padded[1:-1, :-2, 1:-1].astype(jnp.float32)
    z_next = padded[1:-1, 1:-1, 2:].astype(jnp.float32)
    z_prev = padded[1:-1, 1:-1, :-2].astype(jnp.float32)
    spread = x_next + x_prev + y_next + y_prev + z_next + z_prev - 6.0 * center
    carried = velocity[0] * (x_next * x_next - x_prev * x_prev)
    carried = carried + velocity[1] * (y_next * y_next - y_prev * y_prev)
    carried = carried + velocity[2] * (z_next * z_next - z_prev * z_prev)
    result = kappa[..., None] * spread - 0.25 * carried
    return result.astype(jnp.bfloat16)

def reference(basis, kappa, velocity, coefficients, propagator):
    scale = 1.0 / jnp.sqrt(jnp.float32(NX * NY * NZ))
    state = coefficients
    block_ids = jnp.arange(N_WIDE).astype(jnp.int32)
    for step in range(ITERS):
        lift_rows = state.astype(jnp.bfloat16)

        def lift_block(index):
            rows = lax.dynamic_slice_in_dim(basis, index * CX, CX, 0).reshape(CX * NY * NZ, R)
            made = lax.dot_general(rows, lift_rows, (((1,), (1,)), ((), ())), preferred_element_type=jnp.float32)
            return made.astype(jnp.bfloat16)
        lifted = lax.map(lift_block, block_ids).reshape(NX, NY, NZ, P_SIZE)
        padded = jnp.pad(lifted, ((1, 1), (1, 1), (1, 1), (0, 0)))

        def project_block(total, index):
            window = lax.dynamic_slice_in_dim(padded, index * CX, CX + 2, 0)
            local_kappa = lax.dynamic_slice_in_dim(kappa, index * CX, CX, 0)
            forcing = forcing_of(window, local_kappa, velocity).reshape(CX * NY * NZ, P_SIZE)
            rows = lax.dynamic_slice_in_dim(basis, index * CX, CX, 0).reshape(CX * NY * NZ, R)
            term = lax.dot_general(forcing, rows, (((0,), (0,)), ((), ())), preferred_element_type=jnp.float32)
            return (total + term, None)
        total, unused = lax.scan(project_block, jnp.zeros((P_SIZE, R), jnp.float32), block_ids)
        projected = total * scale
        update = state + step_size * projected
        state = update + jnp.dot(update, propagator.T, precision=lax.Precision.HIGHEST, preferred_element_type=jnp.float32)
    return state
```

```python
import functools
import math

import jax
import jax.numpy as jnp
from jax import lax
from jax.experimental import pallas as pl
from jax.experimental.pallas import tpu as pltpu
from jax.sharding import PartitionSpec as P

ITERS = 2
STEP_SIZE = 4.0
F32 = jnp.float32
BF16 = jnp.bfloat16
NT = (((1,), (1,)), ((), ()))
TN = (((0,), (0,)), ((), ()))


def swap(x, axis, distance):
    devices = lax.axis_size(axis)
    return lax.ppermute(x, axis, [(i, i ^ distance) for i in range(devices)])


def gather(x, axis):
    blocks = {0: x}
    distance = lax.axis_size(axis) // 2
    while distance:
        blocks.update({r | distance: swap(block, axis, distance) for r, block in list(blocks.items())})
        distance //= 2
    return [blocks[r] for r in range(len(blocks))]


def split(x):
    high = x.astype(BF16)
    return high, (x - high.astype(F32)).astype(BF16)


def apply_propagator(update, high_ref, low_ref):
    high, low = split(update)
    made = lax.dot_general(high, high_ref[...], NT, preferred_element_type=F32)
    made += lax.dot_general(high, low_ref[...], NT, preferred_element_type=F32)
    made += lax.dot_general(low, high_ref[...], NT, preferred_element_type=F32)
    return update + made


def project(state, place_ref, mains, halos, kappas, velocity_ref, dims, pair_ref, lifted_ref, kappa_ref, forcing_ref):
    size_y, size_x, samples, modes = dims
    wide = len(mains)
    span = wide * size_x
    lanes = 2 * samples
    rounded = state.astype(BF16)
    nothing = jnp.zeros((samples, modes), BF16)
    pair_ref[pl.ds(0, samples), pl.ds(0, modes)] = rounded
    pair_ref[pl.ds(0, samples), pl.ds(modes, modes)] = nothing
    pair_ref[pl.ds(samples, samples), pl.ds(0, modes)] = nothing
    pair_ref[pl.ds(samples, samples), pl.ds(modes, modes)] = rounded
    pair = pair_ref[...]
    lower = lax.broadcasted_iota(jnp.int32, (size_y * size_x, lanes), 1) < samples
    starts = []
    for r in range(wide):
        start = pl.multiple_of((place_ref[0] ^ r) * size_x, size_x)
        starts.append(start)
        rows = pl.ds(start, size_x)
        made = lax.dot_general(mains[r][...], pair, NT, preferred_element_type=F32).astype(BF16).astype(F32)
        lifted_ref[pl.ds(1, size_y), rows, :] = made.reshape(size_y, size_x, lanes)
        made = lax.dot_general(halos[r][...], pair, NT, preferred_element_type=F32).astype(BF16).astype(F32)
        lifted_ref[0, rows, :] = made[:size_x]
        lifted_ref[size_y + 1, rows, :] = made[size_x:]
        cells = jnp.where(lower, kappas[r][:, 0:1], kappas[r][:, 1:2])
        kappa_ref[:, rows, :] = cells.reshape(size_y, size_x, lanes)
    place = lax.broadcasted_iota(jnp.int32, (span, lanes), 0)
    first, last = place == 0, place == span - 1
    speed_x, speed_y, speed_z = (velocity_ref[pl.ds(d, 1), :] for d in range(3))
    for y in range(size_y):
        center = lifted_ref[y + 1]
        y_prev, y_next = lifted_ref[y], lifted_ref[y + 2]
        x_prev = jnp.where(first, 0.0, pltpu.roll(center, 1, 0))
        x_next = jnp.where(last, 0.0, pltpu.roll(center, span - 1, 0))
        other = pltpu.roll(center, samples, 1)
        spread = x_next + x_prev + y_next + y_prev + other - 6.0 * center
        carried = speed_x * (x_next * x_next - x_prev * x_prev)
        carried = carried + speed_y * (y_next * y_next - y_prev * y_prev)
        carried = carried + speed_z * (other * other)
        forcing_ref[y] = (kappa_ref[y] * spread - carried).astype(BF16)
    total = None
    for r in range(wide):
        forcing = forcing_ref[:, pl.ds(starts[r], size_x), :].reshape(size_y * size_x, lanes)
        turned = forcing.T
        for z in range(2):
            made = jnp.dot(
                turned[z * samples : (z + 1) * samples],
                mains[r][:, pl.ds(z * modes, modes)],
                preferred_element_type=F32,
            )
            total = made if total is None else total + made
    return total


def first_kernel(dims, wide, place_ref, *refs):
    mains, halos, kappas = (refs[i * wide : (i + 1) * wide] for i in range(3))
    velocity_ref, state_ref, total_ref, sent_ref = refs[3 * wide : 3 * wide + 4]
    total = project(state_ref[...], place_ref, mains, halos, kappas, velocity_ref, dims, *refs[3 * wide + 4 :])
    total_ref[...] = total
    sent_ref[...] = total.astype(BF16)


def next_kernel(dims, wide, factor, half, place_ref, *refs):
    mains, halos, kappas = (refs[i * wide : (i + 1) * wide] for i in range(3))
    velocity_ref, state_ref, high_ref, low_ref, mine_ref, other_ref, new_ref, kept_ref, sent_ref = refs[3 * wide : 3 * wide + 9]
    update = state_ref[...] + factor * (mine_ref[...] + other_ref[...].astype(F32))
    state = apply_propagator(update, high_ref, low_ref)
    new_ref[...] = state
    total_ref = refs[-1]
    total_ref[...] = project(state, place_ref, mains, halos, kappas, velocity_ref, dims, *refs[3 * wide + 9 : -1])
    kept_ref[...] = total_ref[pl.ds(pl.multiple_of(place_ref[1] * half, half), half), :]
    sent_ref[...] = total_ref[pl.ds(pl.multiple_of((1 - place_ref[1]) * half, half), half), :].astype(BF16)


def last_kernel(factor, state_ref, high_ref, low_ref, mine_ref, other_ref, out_ref):
    update = state_ref[...] + factor * (mine_ref[...] + other_ref[...].astype(F32))
    out_ref[...] = apply_propagator(update, high_ref, low_ref)


def body(basis, kappa, velocity, coefficients, propagator):
    size_x, size_y, size_z, modes = basis.shape
    columns = coefficients.shape[0]
    wide, narrow = lax.axis_size("wide"), lax.axis_size("narrow")
    owned = columns // (wide * narrow)
    real = owned * narrow
    samples = -(-real // 64) * 64
    factor = STEP_SIZE / math.sqrt(size_x * size_y * size_z * wide * narrow)
    w, n = lax.axis_index("wide"), lax.axis_index("narrow")

    cells = basis.transpose(1, 0, 2, 3).reshape(size_y, size_x, size_z * modes)
    up = [(i, i + 1) for i in range(narrow - 1)]
    down = [(j, i) for i, j in up]
    mains = gather(cells.reshape(size_y * size_x, size_z * modes), "wide")
    halo = jnp.concatenate(
        [lax.ppermute(cells[size_y - 1], "narrow", up), lax.ppermute(cells[0], "narrow", down)], axis=0
    )
    halos = gather(halo, "wide")
    kappas = gather(kappa.transpose(1, 0, 2).reshape(size_y * size_x, size_z), "wide")

    def padded(x):
        return x if real == samples else jnp.pad(x, ((0, samples - real), (0, 0)))

    state = padded(lax.dynamic_slice_in_dim(coefficients, w * real, real, 0))
    speed = 0.25 * lax.dynamic_slice_in_dim(velocity, w * real, real, 1)
    if real != samples:
        speed = jnp.pad(speed, ((0, 0), (0, samples - real)))
    speed = jnp.concatenate([speed, speed * jnp.array([[1.0], [1.0], [-1.0]], F32)], axis=1)
    high = lax.reduce_precision(propagator, 8, 7)
    low = (propagator - high).astype(BF16)
    high = high.astype(BF16)

    dims = (size_y, size_x, samples, modes)
    span = wide * size_x
    scratch = [
        pltpu.VMEM((2 * samples, size_z * modes), BF16),
        pltpu.VMEM((size_y + 2, span, 2 * samples), F32),
        pltpu.VMEM((size_y, span, 2 * samples), F32),
        pltpu.VMEM((size_y, span, 2 * samples), BF16),
    ]
    smem = pl.BlockSpec(memory_space=pltpu.SMEM)
    vmem = pl.BlockSpec(memory_space=pltpu.VMEM)
    half = real // 2
    top = narrow // 2
    place = jnp.stack([w, n // top]).astype(jnp.int32)
    fixed = (*mains, *halos, *kappas, speed)

    total, sent = pl.pallas_call(
        functools.partial(first_kernel, dims, wide),
        out_shape=(jax.ShapeDtypeStruct((samples, modes), F32), jax.ShapeDtypeStruct((samples, modes), BF16)),
        in_specs=[smem] + [vmem] * (len(fixed) + 1),
        out_specs=(vmem, vmem),
        scratch_shapes=scratch,
    )(place, *fixed, state)
    distance = 1
    while distance < top:
        total = total + swap(sent, "narrow", distance).astype(F32)
        sent = total.astype(BF16)
        distance *= 2
    got = swap(sent, "narrow", top)
    state, total, sent = pl.pallas_call(
        functools.partial(next_kernel, dims, wide, factor, half),
        out_shape=(
            jax.ShapeDtypeStruct((samples, modes), F32),
            jax.ShapeDtypeStruct((half, modes), F32),
            jax.ShapeDtypeStruct((half, modes), BF16),
        ),
        in_specs=[smem] + [vmem] * (len(fixed) + 5),
        out_specs=(vmem, vmem, vmem),
        scratch_shapes=scratch + [pltpu.VMEM((samples, modes), F32)],
    )(place, *fixed, state, high, low, total, got)
    distance = top
    while distance > 1:
        total = total + swap(sent, "narrow", distance).astype(F32)
        distance //= 2
        rows = total.shape[0] // 2
        bit = (n // distance) % 2
        sent = lax.dynamic_slice_in_dim(total, (1 - bit) * rows, rows, 0).astype(BF16)
        total = lax.dynamic_slice_in_dim(total, bit * rows, rows, 0)
    got = swap(sent, "narrow", 1)
    state = lax.dynamic_slice_in_dim(state, n * owned, owned, 0)
    room = max(owned, 16)
    state, total, got = (
        x if room == owned else jnp.pad(x, ((0, room - owned), (0, 0))) for x in (state, total, got)
    )
    out = pl.pallas_call(
        functools.partial(last_kernel, factor),
        out_shape=jax.ShapeDtypeStruct((room, modes), F32),
        in_specs=[vmem] * 5,
        out_specs=vmem,
    )(state, high, low, total, got)
    return out[:owned]


def solution(mesh):
    placed = (
        P(("groups", "wide"), "narrow", None, None),
        P(("groups", "wide"), "narrow", None),
        P(None, "groups"),
        P("groups", None),
        P("groups", None),
    )
    return jax.shard_map(
        body,
        mesh=mesh,
        in_specs=placed,
        out_specs=P(("groups", "wide", "narrow"), None),
        check_vma=False,
    )
```

```python
import functools
import math

import jax
import jax.numpy as jnp
from jax import lax
from jax.experimental import pallas as pl
from jax.experimental.pallas import tpu as pltpu
from jax.sharding import PartitionSpec as P

ROOM = pltpu.CompilerParams(vmem_limit_bytes=24 * 1024 * 1024)
STEP_SIZE = 4.0
F32 = jnp.float32
BF16 = jnp.bfloat16
NT = (((1,), (1,)), ((), ()))
TN = (((0,), (0,)), ((), ()))


def swap(x, axis, distance):
    devices = lax.axis_size(axis)
    return lax.ppermute(x, axis, [(i, i ^ distance) for i in range(devices)])


def gather(x, axis):
    blocks = {0: x}
    distance = lax.axis_size(axis) // 2
    while distance:
        blocks.update({r | distance: swap(block, axis, distance) for r, block in list(blocks.items())})
        distance //= 2
    return [blocks[r] for r in range(len(blocks))]


def split(x):
    high = x.astype(BF16)
    return high, (x - high.astype(F32)).astype(BF16)


def apply_propagator(update, high_ref, low_ref):
    high, low = split(update)
    made = lax.dot_general(high, high_ref[...], NT, preferred_element_type=F32)
    made += lax.dot_general(high, low_ref[...], NT, preferred_element_type=F32)
    made += lax.dot_general(low, high_ref[...], NT, preferred_element_type=F32)
    return update + made


def project(state, place_ref, mains, halos, kappas, velocity_ref, dims, pair_ref, lifted_ref, kappa_ref, forcing_ref):
    size_y, size_x, samples, modes = dims
    wide = len(mains)
    span = wide * size_x
    lanes = 2 * samples
    rounded = state.astype(BF16)
    nothing = jnp.zeros((samples, modes), BF16)
    pair_ref[pl.ds(0, samples), pl.ds(0, modes)] = rounded
    pair_ref[pl.ds(0, samples), pl.ds(modes, modes)] = nothing
    pair_ref[pl.ds(samples, samples), pl.ds(0, modes)] = nothing
    pair_ref[pl.ds(samples, samples), pl.ds(modes, modes)] = rounded
    pair = pair_ref[...]
    lower = lax.broadcasted_iota(jnp.int32, (size_y * size_x, lanes), 1) < samples
    starts = []
    for r in range(wide):
        start = pl.multiple_of((place_ref[0] ^ r) * size_x, size_x)
        starts.append(start)
        rows = pl.ds(start, size_x)
        made = lax.dot_general(mains[r][...], pair, NT, preferred_element_type=F32).astype(BF16).astype(F32)
        lifted_ref[pl.ds(1, size_y), rows, :] = made.reshape(size_y, size_x, lanes)
        made = lax.dot_general(halos[r][...], pair, NT, preferred_element_type=F32).astype(BF16).astype(F32)
        lifted_ref[0, rows, :] = made[:size_x]
        lifted_ref[size_y + 1, rows, :] = made[size_x:]
        cells = jnp.where(lower, kappas[r][:, 0:1], kappas[r][:, 1:2])
        kappa_ref[:, rows, :] = cells.reshape(size_y, size_x, lanes)
    place = lax.broadcasted_iota(jnp.int32, (span, lanes), 0)
    first, last = place == 0, place == span - 1
    speed_x, speed_y, speed_z = (velocity_ref[pl.ds(d, 1), :] for d in range(3))
    for y in range(size_y):
        center = lifted_ref[y + 1]
        y_prev, y_next = lifted_ref[y], lifted_ref[y + 2]
        x_prev = jnp.where(first, 0.0, pltpu.roll(center, 1, 0))
        x_next = jnp.where(last, 0.0, pltpu.roll(center, span - 1, 0))
        other = pltpu.roll(center, samples, 1)
        spread = x_next + x_prev + y_next + y_prev + other - 6.0 * center
        carried = speed_x * (x_next * x_next - x_prev * x_prev)
        carried = carried + speed_y * (y_next * y_next - y_prev * y_prev)
        carried = carried + speed_z * (other * other)
        forcing_ref[y] = (kappa_ref[y] * spread - carried).astype(BF16)
    total = None
    for r in range(wide):
        forcing = forcing_ref[:, pl.ds(starts[r], size_x), :].reshape(size_y * size_x, lanes)
        turned = forcing.T
        for z in range(2):
            made = jnp.dot(
                turned[z * samples : (z + 1) * samples],
                mains[r][:, pl.ds(z * modes, modes)],
                preferred_element_type=F32,
            )
            total = made if total is None else total + made
    return total


def first_kernel(dims, wide, place_ref, *refs):
    mains, halos, kappas = (refs[i * wide : (i + 1) * wide] for i in range(3))
    velocity_ref, state_ref, total_ref, sent_ref = refs[3 * wide : 3 * wide + 4]
    total = project(state_ref[...], place_ref, mains, halos, kappas, velocity_ref, dims, *refs[3 * wide + 4 :])
    total_ref[...] = total
    sent_ref[...] = total.astype(BF16)


def next_kernel(dims, wide, factor, half, place_ref, *refs):
    mains, halos, kappas = (refs[i * wide : (i + 1) * wide] for i in range(3))
    velocity_ref, state_ref, high_ref, low_ref, mine_ref, other_ref, new_ref, kept_ref, sent_ref = refs[3 * wide : 3 * wide + 9]
    update = state_ref[...] + factor * (mine_ref[...] + other_ref[...].astype(F32))
    state = apply_propagator(update, high_ref, low_ref)
    new_ref[...] = state
    total_ref = refs[-1]
    total_ref[...] = project(state, place_ref, mains, halos, kappas, velocity_ref, dims, *refs[3 * wide + 9 : -1])
    kept_ref[...] = total_ref[pl.ds(pl.multiple_of(place_ref[1] * half, half), half), :]
    sent_ref[...] = total_ref[pl.ds(pl.multiple_of((1 - place_ref[1]) * half, half), half), :].astype(BF16)


def last_kernel(factor, state_ref, high_ref, low_ref, mine_ref, other_ref, out_ref):
    update = state_ref[...] + factor * (mine_ref[...] + other_ref[...].astype(F32))
    out_ref[...] = apply_propagator(update, high_ref, low_ref)


def body(basis, kappa, velocity, coefficients, propagator):
    size_x, size_y, size_z, modes = basis.shape
    columns = coefficients.shape[0]
    wide, narrow = lax.axis_size("wide"), lax.axis_size("narrow")
    owned = columns // (wide * narrow)
    real = owned * narrow
    samples = -(-real // 64) * 64
    factor = STEP_SIZE / math.sqrt(size_x * size_y * size_z * wide * narrow)
    w, n = lax.axis_index("wide"), lax.axis_index("narrow")

    cells = basis.transpose(1, 0, 2, 3).reshape(size_y, size_x, size_z * modes)
    up = [(i, i + 1) for i in range(narrow - 1)]
    down = [(j, i) for i, j in up]
    mains = gather(cells.reshape(size_y * size_x, size_z * modes), "wide")
    halo = jnp.concatenate(
        [lax.ppermute(cells[size_y - 1], "narrow", up), lax.ppermute(cells[0], "narrow", down)], axis=0
    )
    halos = gather(halo, "wide")
    kappas = gather(kappa.transpose(1, 0, 2).reshape(size_y * size_x, size_z), "wide")

    def padded(x):
        return x if real == samples else jnp.pad(x, ((0, samples - real), (0, 0)))

    state = padded(lax.dynamic_slice_in_dim(coefficients, w * real, real, 0))
    speed = 0.25 * lax.dynamic_slice_in_dim(velocity, w * real, real, 1)
    if real != samples:
        speed = jnp.pad(speed, ((0, 0), (0, samples - real)))
    speed = jnp.concatenate([speed, speed * jnp.array([[1.0], [1.0], [-1.0]], F32)], axis=1)
    high = lax.reduce_precision(propagator, 8, 7)
    low = (propagator - high).astype(BF16)
    high = high.astype(BF16)

    dims = (size_y, size_x, samples, modes)
    span = wide * size_x
    scratch = [
        pltpu.VMEM((2 * samples, size_z * modes), BF16),
        pltpu.VMEM((size_y + 2, span, 2 * samples), F32),
        pltpu.VMEM((size_y, span, 2 * samples), F32),
        pltpu.VMEM((size_y, span, 2 * samples), BF16),
    ]
    smem = pl.BlockSpec(memory_space=pltpu.SMEM)
    vmem = pl.BlockSpec(memory_space=pltpu.VMEM)
    half = real // 2
    top = narrow // 2
    place = jnp.stack([w, n // top]).astype(jnp.int32)
    fixed = (*mains, *halos, *kappas, speed)

    total, sent = pl.pallas_call(
        functools.partial(first_kernel, dims, wide),
        out_shape=(jax.ShapeDtypeStruct((samples, modes), F32), jax.ShapeDtypeStruct((samples, modes), BF16)),
        in_specs=[smem] + [vmem] * (len(fixed) + 1),
        out_specs=(vmem, vmem),
        scratch_shapes=scratch,
        compiler_params=ROOM,
    )(place, *fixed, state)
    distance = 1
    while distance < top:
        total = total + swap(sent, "narrow", distance).astype(F32)
        sent = total.astype(BF16)
        distance *= 2
    got = swap(sent, "narrow", top)
    state, total, sent = pl.pallas_call(
        functools.partial(next_kernel, dims, wide, factor, half),
        out_shape=(
            jax.ShapeDtypeStruct((samples, modes), F32),
            jax.ShapeDtypeStruct((half, modes), F32),
            jax.ShapeDtypeStruct((half, modes), BF16),
        ),
        in_specs=[smem] + [vmem] * (len(fixed) + 5),
        out_specs=(vmem, vmem, vmem),
        scratch_shapes=scratch + [pltpu.VMEM((samples, modes), F32)],
        compiler_params=ROOM,
    )(place, *fixed, state, high, low, total, got)
    distance = top
    while distance > 1:
        total = total + swap(sent, "narrow", distance).astype(F32)
        distance //= 2
        rows = total.shape[0] // 2
        bit = (n // distance) % 2
        sent = lax.dynamic_slice_in_dim(total, (1 - bit) * rows, rows, 0).astype(BF16)
        total = lax.dynamic_slice_in_dim(total, bit * rows, rows, 0)
    got = swap(sent, "narrow", 1)
    state = lax.dynamic_slice_in_dim(state, n * owned, owned, 0)
    room = max(owned, 16)
    state, total, got = (
        x if room == owned else jnp.pad(x, ((0, room - owned), (0, 0))) for x in (state, total, got)
    )
    out = pl.pallas_call(
        functools.partial(last_kernel, factor),
        out_shape=jax.ShapeDtypeStruct((room, modes), F32),
        in_specs=[vmem] * 5,
        out_specs=vmem,
        compiler_params=ROOM,
    )(state, high, low, total, got)
    return out[:owned]


def solution(mesh):
    placed = (
        P(("groups", "wide"), "narrow", None, None),
        P(("groups", "wide"), "narrow", None),
        P(None, "groups"),
        P("groups", None),
        P("groups", None),
    )
    return jax.shard_map(
        body,
        mesh=mesh,
        in_specs=placed,
        out_specs=P(("groups", "wide", "narrow"), None),
        check_vma=False,
    )
```

```python
import functools
import math

import jax
import jax.numpy as jnp
from jax import lax
from jax.experimental import pallas as pl
from jax.experimental.pallas import tpu as pltpu
from jax.sharding import PartitionSpec as P

ROOM = pltpu.CompilerParams(vmem_limit_bytes=24 * 1024 * 1024)
STEP_SIZE = 4.0
F32 = jnp.float32
BF16 = jnp.bfloat16
NT = (((1,), (1,)), ((), ()))
TN = (((0,), (0,)), ((), ()))


def swap(x, axis, distance):
    devices = lax.axis_size(axis)
    return lax.ppermute(x, axis, [(i, i ^ distance) for i in range(devices)])


def split(x):
    high = x.astype(BF16)
    return high, (x - high.astype(F32)).astype(BF16)


def apply_propagator(update, high_ref, low_ref):
    high, low = split(update)
    made = lax.dot_general(high, high_ref[...], NT, preferred_element_type=F32)
    made += lax.dot_general(high, low_ref[...], NT, preferred_element_type=F32)
    made += lax.dot_general(low, high_ref[...], NT, preferred_element_type=F32)
    return update + made


def project(state, place_ref, mains, halos, kappas, velocity_ref, dims, pair_ref, lifted_ref, kappa_ref, forcing_ref):
    size_y, size_x, samples, modes = dims
    wide = len(mains)
    span = wide * size_x
    lanes = 2 * samples
    rounded = state.astype(BF16)
    nothing = jnp.zeros((samples, modes), BF16)
    pair_ref[pl.ds(0, samples), pl.ds(0, modes)] = rounded
    pair_ref[pl.ds(0, samples), pl.ds(modes, modes)] = nothing
    pair_ref[pl.ds(samples, samples), pl.ds(0, modes)] = nothing
    pair_ref[pl.ds(samples, samples), pl.ds(modes, modes)] = rounded
    pair = pair_ref[...]
    lower = lax.broadcasted_iota(jnp.int32, (size_y * size_x, lanes), 1) < samples
    starts = []
    for r in range(wide):
        start = pl.multiple_of((place_ref[0] ^ r) * size_x, size_x)
        starts.append(start)
        rows = pl.ds(start, size_x)
        made = lax.dot_general(mains[r][...], pair, NT, preferred_element_type=F32).astype(BF16).astype(F32)
        lifted_ref[pl.ds(1, size_y), rows, :] = made.reshape(size_y, size_x, lanes)
        made = lax.dot_general(halos[r][...], pair, NT, preferred_element_type=F32).astype(BF16).astype(F32)
        lifted_ref[0, rows, :] = made[:size_x]
        lifted_ref[size_y + 1, rows, :] = made[size_x:]
        cells = jnp.where(lower, kappas[r][:, 0:1], kappas[r][:, 1:2])
        kappa_ref[:, rows, :] = cells.reshape(size_y, size_x, lanes)
    place = lax.broadcasted_iota(jnp.int32, (span, lanes), 0)
    first, last = place == 0, place == span - 1
    speed_x, speed_y, speed_z = (velocity_ref[pl.ds(d, 1), :] for d in range(3))
    for y in range(size_y):
        center = lifted_ref[y + 1]
        y_prev, y_next = lifted_ref[y], lifted_ref[y + 2]
        x_prev = jnp.where(first, 0.0, pltpu.roll(center, 1, 0))
        x_next = jnp.where(last, 0.0, pltpu.roll(center, span - 1, 0))
        other = pltpu.roll(center, samples, 1)
        spread = x_next + x_prev + y_next + y_prev + other - 6.0 * center
        carried = speed_x * (x_next * x_next - x_prev * x_prev)
        carried = carried + speed_y * (y_next * y_next - y_prev * y_prev)
        carried = carried + speed_z * (other * other)
        forcing_ref[y] = (kappa_ref[y] * spread - carried).astype(BF16)
    total = None
    for r in range(wide):
        forcing = forcing_ref[:, pl.ds(starts[r], size_x), :].reshape(size_y * size_x, lanes)
        turned = forcing.T
        for z in range(2):
            made = jnp.dot(
                turned[z * samples : (z + 1) * samples],
                mains[r][:, pl.ds(z * modes, modes)],
                preferred_element_type=F32,
            )
            total = made if total is None else total + made
    return total


def turn_kernel(basis_ref, out_ref, sem):
    copies = [pltpu.make_async_copy(basis_ref.at[:, y], out_ref.at[y], sem.at[y]) for y in range(out_ref.shape[0])]
    for copy in copies:
        copy.start()
    for copy in copies:
        copy.wait()


def first_kernel(dims, wide, place_ref, *refs):
    fixed = 3 * wide + 2
    mains, halos, kappas = (refs[i * wide : (i + 1) * wide] for i in range(3))
    velocity_ref, state_ref = refs[3 * wide : fixed]
    total_ref, sent_ref = refs[2 * fixed : 2 * fixed + 2]
    total = project(state_ref[...], place_ref, mains, halos, kappas, velocity_ref, dims, *refs[2 * fixed + 2 :])
    total_ref[...] = total
    sent_ref[...] = total.astype(BF16)


def next_kernel(dims, wide, narrow, factor, owned, place_ref, *refs):
    mains, halos, kappas = (refs[i * wide : (i + 1) * wide] for i in range(3))
    velocity_ref, state_ref, high_ref, low_ref, mine_ref = refs[3 * wide : 3 * wide + 5]
    others, refs = refs[3 * wide + 5 : 3 * wide + 4 + narrow], refs[3 * wide + 4 + narrow :]
    new_ref, kept_ref, sent, refs = refs[0], refs[1], refs[2 : narrow + 1], refs[narrow + 1 :]
    total_ref, fresh_ref = refs[-2:]
    total = mine_ref[...]
    for other_ref in others:
        total = total + other_ref[...].astype(F32)
    state = apply_propagator(state_ref[...] + factor * total, high_ref, low_ref)
    fresh_ref[...] = state
    total_ref[...] = project(state, place_ref, mains, halos, kappas, velocity_ref, dims, *refs[:-2])

    def rows(distance):
        start = (place_ref[1] ^ distance) * owned
        return pl.ds(pl.multiple_of(start, owned), owned)

    new_ref[...] = fresh_ref[rows(0), :]
    kept_ref[...] = total_ref[rows(0), :]
    for distance in range(1, narrow):
        sent[distance - 1][...] = total_ref[rows(distance), :].astype(BF16)


def last_kernel(factor, state_ref, high_ref, low_ref, mine_ref, *refs):
    total = mine_ref[...]
    for other_ref in refs[:-1]:
        total = total + other_ref[...].astype(F32)
    refs[-1][...] = apply_propagator(state_ref[...] + factor * total, high_ref, low_ref)


def body(basis, kappa, velocity, coefficients, propagator):
    size_x, size_y, size_z, modes = basis.shape
    columns = coefficients.shape[0]
    wide, narrow = lax.axis_size("wide"), lax.axis_size("narrow")
    owned = columns // (wide * narrow)
    real = owned * narrow
    samples = -(-real // 64) * 64
    factor = STEP_SIZE / math.sqrt(size_x * size_y * size_z * wide * narrow)
    w, n = lax.axis_index("wide"), lax.axis_index("narrow")
    smem = pl.BlockSpec(memory_space=pltpu.SMEM)
    vmem = pl.BlockSpec(memory_space=pltpu.VMEM)

    turned = pl.pallas_call(
        turn_kernel,
        out_shape=jax.ShapeDtypeStruct((size_y, size_x, size_z, modes), BF16),
        in_specs=[pl.BlockSpec(memory_space=pl.ANY)],
        out_specs=vmem,
        scratch_shapes=[pltpu.SemaphoreType.DMA((size_y,))],
        compiler_params=ROOM,
    )(basis)
    cells = turned.reshape(size_y, size_x, size_z * modes)
    up = [(i, i + 1) for i in range(narrow - 1)]
    down = [(j, i) for i, j in up]
    main = cells.reshape(size_y * size_x, size_z * modes)
    halo = jnp.concatenate(
        [lax.ppermute(cells[size_y - 1], "narrow", up), lax.ppermute(cells[0], "narrow", down)], axis=0
    )
    cell_kappa = kappa.transpose(1, 0, 2).reshape(size_y * size_x, size_z)
    blocks = {0: (main, halo, cell_kappa)}
    distance = wide // 2
    while distance:
        found = {r | distance: tuple(swap(x, "wide", distance) for x in block) for r, block in blocks.items()}
        if distance > 1:
            found = {r: lax.optimization_barrier(block) for r, block in found.items()}
        blocks.update(found)
        distance //= 2
    mains, halos, kappas = zip(*(blocks[r] for r in range(wide)))

    def padded(x):
        return x if real == samples else jnp.pad(x, ((0, samples - real), (0, 0)))

    state = padded(lax.dynamic_slice_in_dim(coefficients, w * real, real, 0))
    speed = 0.25 * lax.dynamic_slice_in_dim(velocity, w * real, real, 1)
    if real != samples:
        speed = jnp.pad(speed, ((0, 0), (0, samples - real)))
    speed = jnp.concatenate([speed, speed * jnp.array([[1.0], [1.0], [-1.0]], F32)], axis=1)
    high = lax.reduce_precision(propagator, 8, 7)
    low = (propagator - high).astype(BF16)
    high = high.astype(BF16)

    dims = (size_y, size_x, samples, modes)
    span = wide * size_x
    scratch = [
        pltpu.VMEM((2 * samples, size_z * modes), BF16),
        pltpu.VMEM((size_y + 2, span, 2 * samples), F32),
        pltpu.VMEM((size_y, span, 2 * samples), F32),
        pltpu.VMEM((size_y, span, 2 * samples), BF16),
    ]
    place = jnp.stack([w, n]).astype(jnp.int32)
    fixed = (*mains, *halos, *kappas, speed, state)

    *fixed, total, sent = pl.pallas_call(
        functools.partial(first_kernel, dims, wide),
        out_shape=[jax.ShapeDtypeStruct(x.shape, x.dtype) for x in fixed]
        + [jax.ShapeDtypeStruct((samples, modes), F32), jax.ShapeDtypeStruct((samples, modes), BF16)],
        in_specs=[smem] + [vmem] * len(fixed),
        out_specs=[vmem] * (len(fixed) + 2),
        scratch_shapes=scratch,
        input_output_aliases={i + 1: i for i in range(len(fixed))},
        compiler_params=ROOM,
    )(place, *fixed)
    others = [swap(sent, "narrow", distance) for distance in range(1, narrow)]
    piece = (owned, modes)
    state, total, *sent = pl.pallas_call(
        functools.partial(next_kernel, dims, wide, narrow, factor, owned),
        out_shape=[jax.ShapeDtypeStruct(piece, F32)] * 2 + [jax.ShapeDtypeStruct(piece, BF16)] * (narrow - 1),
        in_specs=[smem] + [vmem] * (len(fixed) + 2 + narrow),
        out_specs=[vmem] * (narrow + 1),
        scratch_shapes=scratch + [pltpu.VMEM((samples, modes), F32)] * 2,
        compiler_params=ROOM,
    )(place, *fixed, high, low, total, *others)
    others = [swap(x, "narrow", distance + 1) for distance, x in enumerate(sent)]
    room = max(owned, 16)
    parts = [x if room == owned else jnp.pad(x, ((0, room - owned), (0, 0))) for x in (state, total, *others)]
    out = pl.pallas_call(
        functools.partial(last_kernel, factor),
        out_shape=jax.ShapeDtypeStruct((room, modes), F32),
        in_specs=[vmem] * (3 + narrow),
        out_specs=vmem,
        compiler_params=ROOM,
    )(parts[0], high, low, *parts[1:])
    return out[:owned]


def solution(mesh):
    placed = (
        P(("groups", "wide"), "narrow", None, None),
        P(("groups", "wide"), "narrow", None),
        P(None, "groups"),
        P("groups", None),
        P("groups", None),
    )
    return jax.shard_map(
        body,
        mesh=mesh,
        in_specs=placed,
        out_specs=P(("groups", "wide", "narrow"), None),
        check_vma=False,
    )
```

```python
import functools
import math

import jax
import jax.numpy as jnp
from jax import lax
from jax.experimental import pallas as pl
from jax.experimental.pallas import tpu as pltpu
from jax.sharding import PartitionSpec as P


ROOM = pltpu.CompilerParams(vmem_limit_bytes=24 * 1024 * 1024)
STEP_SIZE = 4.0
F32 = jnp.float32
BF16 = jnp.bfloat16
NT = (((1,), (1,)), ((), ()))
TN = (((0,), (0,)), ((), ()))
KAPPA_ROWS = 8


def swap(x, axis, distance):
    return lax.ppermute(x, axis, [(i, i ^ distance) for i in range(lax.axis_size(axis))])


def split(x):
    high = x.astype(BF16)
    return high, (x - high.astype(F32)).astype(BF16)


def apply_propagator(update, high_ref, low_ref):
    rows = update.shape[0]
    high, low = split(update)
    made = lax.dot_general(jnp.concatenate([high, low], axis=0), high_ref[...], NT, preferred_element_type=F32)
    made = made[:rows] + made[rows:]
    return update + (made + lax.dot_general(high, low_ref[...], NT, preferred_element_type=F32))


def place_state(state, pair_ref):
    samples, modes = state.shape
    rounded = state.astype(BF16)
    nothing = jnp.zeros((samples, modes), BF16)
    pair_ref[pl.ds(0, samples), pl.ds(0, modes)] = rounded
    pair_ref[pl.ds(0, samples), pl.ds(modes, modes)] = nothing
    pair_ref[pl.ds(samples, samples), pl.ds(0, modes)] = nothing
    pair_ref[pl.ds(samples, samples), pl.ds(modes, modes)] = rounded


def lift(todo, pair_ref):
    pair = pair_ref[...]
    for at in range(0, len(todo), 12):
        group = todo[at : at + 12]
        rows = jnp.concatenate([ref[pl.ds(start, count), :] for (ref, start, count), _ in group], axis=0)
        made = lax.dot_general(rows, pair, NT, preferred_element_type=F32).astype(BF16).astype(F32)
        start = 0
        for (_, _, count), store in group:
            store(made[start : start + count])
            start += count


def project(blocks, halos, faces, state, velocity_ref, dims, place_ref, scratch):
    size_y, size_x = dims
    samples, modes = state.shape
    pair_ref, lifted_ref, kappa_ref, forcing_ref, face_ref = scratch
    span, lanes = lifted_ref.shape[1], 2 * samples
    place_state(state, pair_ref)
    columns = [pl.ds(pl.multiple_of(column, size_x), size_x) for column, _, _ in blocks]
    todo = []
    for where, (_, parts, _) in zip(columns, blocks):
        first = 1
        for part in parts:
            high = part[2] // size_x

            def store(made, where=where, first=first, high=high):
                lifted_ref[pl.ds(first, high), where, :] = made.reshape(high, size_x, lanes)

            todo.append((part, store))
            first += high
    for column, row, part in halos:

        def store(made, column=column, row=row):
            lifted_ref[row, pl.ds(pl.multiple_of(column, size_x), made.shape[0]), :] = made

        todo.append((part, store))
    for i, part in enumerate(faces):

        def store(made, i=i):
            face_ref[i] = made

        todo.append((part, store))
    lift(todo, pair_ref)

    part = lax.broadcasted_iota(jnp.int32, (KAPPA_ROWS, lanes), 0)
    side = jnp.where(lax.broadcasted_iota(jnp.int32, (KAPPA_ROWS, lanes), 1) < samples, 0, 1)
    layer = jnp.where(part < 3, 0, jnp.where(part < 6, 1, 2))
    ones = jnp.where(layer == side, 1.0, 0.0).astype(BF16)
    for where, (_, _, (ref, start)) in zip(columns, blocks):
        parts = ref[pl.ds(start, KAPPA_ROWS), pl.ds(0, size_y * size_x)]
        cells = lax.dot_general(parts, ones, TN, preferred_element_type=F32)
        kappa_ref[:, where, :] = cells.reshape(size_y, size_x, lanes)

    place = lax.broadcasted_iota(jnp.int32, (span, lanes), 0)
    first, last = place == 0, place == span - 1
    speed_x, speed_y, speed_z = (velocity_ref[pl.ds(d, 1), :] for d in range(3))
    odd = (place_ref[0] // 2 % 2).astype(F32)
    for y in range(size_y):
        center = lifted_ref[y + 1]
        y_prev, y_next = lifted_ref[y], lifted_ref[y + 2]
        before, after = 0.0, 0.0
        if faces:
            near = face_ref[0, pl.ds(y, 1), :]
            before, after = odd * near, (1.0 - odd) * near
        if len(faces) > 1:
            far = face_ref[1, pl.ds(y, 1), :]
            before, after = before + (1.0 - odd) * far, after + odd * far
        x_prev = jnp.where(first, before, pltpu.roll(center, 1, 0))
        x_next = jnp.where(last, after, pltpu.roll(center, span - 1, 0))
        other = pltpu.roll(center, samples, 1)
        x_sum, y_sum = x_next + x_prev, y_next + y_prev
        spread = x_sum + y_sum + (other - 6.0 * center)
        carried = speed_x * (x_next - x_prev) * x_sum + speed_y * (y_next - y_prev) * y_sum
        carried = carried + speed_z * other * other
        forcing_ref[y] = (kappa_ref[y] * spread - carried).astype(BF16)
    total = None
    for where, (_, parts, _) in zip(columns, blocks):
        first = 0
        for ref, start, count in parts:
            high = count // size_x
            forcing = forcing_ref[pl.ds(first, high), where, :].reshape(count, lanes)
            first += high
            turned = forcing.T
            for z in range(2):
                made = jnp.dot(
                    turned[z * samples : (z + 1) * samples],
                    ref[pl.ds(start, count), pl.ds(z * modes, modes)],
                    preferred_element_type=F32,
                )
                total = made if total is None else total + made
    return total


def turn_kernel(basis_ref, out_ref, sem):
    copies = [pltpu.make_async_copy(basis_ref.at[:, y], out_ref.at[y], sem.at[y]) for y in range(out_ref.shape[0])]
    for copy in copies:
        copy.start()
    for copy in copies:
        copy.wait()


def near_records(refs, place_ref, base, dims):
    size_y, size_x = dims
    main, partner, halo, turned_halo, kappa, partner_kappa = refs
    core = place_ref[0] % 2
    cells = size_y * size_x
    blocks = [
        (base + core * size_x, [(main, 0, cells)], (kappa, 0)),
        (base + (1 - core) * size_x, [(partner, 0, cells)], (partner_kappa, 0)),
    ]
    last = size_y + 1
    halos = [(base, core * last, (halo, 0, 2 * size_x)), (base, (1 - core) * last, (turned_halo, 0, 2 * size_x))]
    return blocks, halos


def first_kernel(dims, chips, real, passed, place_ref, *refs):
    near, refs = refs[:passed], refs[passed:]
    faces = len(refs) - (2 + passed + chips + 5)
    faces, refs = refs[:faces], refs[faces:]
    velocity_ref, state_ref = refs[:2]
    total_ref, sent, scratch = refs[2 + passed], refs[3 + passed : 2 + passed + chips], refs[2 + passed + chips :]
    blocks, halos = near_records(near, place_ref, 0, dims)
    faces = [(ref, 0, dims[0]) for ref in faces]
    total = project(blocks, halos, faces, state_ref[...], velocity_ref, dims, place_ref, scratch)
    total_ref[...] = total[:real]
    for j in range(1, chips):
        sent[j - 1][...] = total[j * real : (j + 1) * real].astype(BF16)


def next_kernel(dims, chips, narrow, factor, owned, passed, place_ref, *refs):
    size_y, size_x = dims
    near, refs = refs[:passed], refs[passed:]
    far, refs = refs[: 4 * (chips - 1)], refs[4 * (chips - 1) :]
    velocity_ref, state_ref, high_ref, low_ref, mine_ref = refs[:5]
    others, refs = refs[5 : 4 + narrow], refs[4 + narrow :]
    new_ref, kept_ref, sent, refs = refs[0], refs[1], refs[2 : narrow + 1], refs[narrow + 1 :]
    scratch, (total_ref, fresh_ref) = refs[:5], refs[5:]
    total = mine_ref[...]
    for other_ref in others:
        total = total + other_ref[...].astype(F32)
    state = apply_propagator(state_ref[...] + factor * total, high_ref, low_ref)
    fresh_ref[...] = state

    chip, core = place_ref[0] // 2, place_ref[0] % 2
    blocks, halos = near_records(near, place_ref, chip * 2 * size_x, dims)
    half = size_y * size_x // 2
    for j in range(1, chips):
        base = (chip ^ j) * 2 * size_x
        for k in range(2):
            top, rest = far[4 * (j - 1) + 2 * k : 4 * (j - 1) + 2 * k + 2]
            side = core if k == 0 else 1 - core
            blocks.append((base + side * size_x, [(top, 0, half), (rest, 0, half)], (rest, half + 2 * size_x)))
            halos.append((base, side * (size_y + 1), (rest, half, 2 * size_x)))
    total_ref[...] = project(blocks, halos, [], state, velocity_ref, dims, place_ref, scratch)

    def rows(distance):
        start = (place_ref[1] ^ distance) * owned
        return pl.ds(pl.multiple_of(start, owned), owned)

    new_ref[...] = fresh_ref[rows(0), :]
    kept_ref[...] = total_ref[rows(0), :]
    for distance in range(1, narrow):
        sent[distance - 1][...] = total_ref[rows(distance), :].astype(BF16)


def last_kernel(factor, state_ref, high_ref, low_ref, mine_ref, *refs):
    total = mine_ref[...]
    for other_ref in refs[:-1]:
        total = total + other_ref[...].astype(F32)
    refs[-1][...] = apply_propagator(state_ref[...] + factor * total, high_ref, low_ref)


def body(basis, kappa, velocity, coefficients, propagator):
    size_x, size_y, size_z, modes = basis.shape
    columns = coefficients.shape[0]
    wide, narrow = lax.axis_size("wide"), lax.axis_size("narrow")
    chips = wide // 2
    owned = columns // (wide * narrow)
    real = owned * narrow
    samples = -(-real // 64) * 64
    factor = STEP_SIZE / math.sqrt(size_x * size_y * size_z * wide * narrow)
    w, n = lax.axis_index("wide"), lax.axis_index("narrow")
    chip, core = w // 2, w % 2
    cells, depth = size_y * size_x, size_z * modes
    smem = pl.BlockSpec(memory_space=pltpu.SMEM)
    vmem = pl.BlockSpec(memory_space=pltpu.VMEM)
    dims = (size_y, size_x)

    def turn(block):
        turned = pl.pallas_call(
            turn_kernel,
            out_shape=jax.ShapeDtypeStruct((size_y, size_x, size_z, modes), BF16),
            in_specs=[pl.BlockSpec(memory_space=pl.ANY)],
            out_specs=vmem,
            scratch_shapes=[pltpu.SemaphoreType.DMA((size_y,))],
            compiler_params=ROOM,
        )(block)
        return turned.reshape(cells, depth)

    left = kappa.transpose(2, 1, 0).reshape(size_z, 1, cells)
    parts = []
    for _ in range(3):
        parts.append(lax.reduce_precision(left, 8, 7))
        left = left - parts[-1]
    cell_kappa = jnp.concatenate(parts, axis=1).reshape(3 * size_z, cells).astype(BF16)
    cell_kappa = jnp.pad(cell_kappa, ((0, KAPPA_ROWS - 3 * size_z), (0, 0)))

    partner_raw = swap(basis, "wide", 1)
    main = turn(basis)
    half = cells // 2
    tops = [swap(main[:half], "wide", 2 * j) for j in range(1, chips)]
    partner = turn(partner_raw)

    def row_of(block):
        return lax.dynamic_slice_in_dim(block, (1 - core) * (cells - size_x), size_x, 0)

    def ordered(mine, other):
        return jnp.where(core == 0, jnp.concatenate([mine, other], axis=0), jnp.concatenate([other, mine], axis=0))

    pairs = [(i * narrow + k, i * narrow + k + 1) for i in range(0, wide, 2) for k in range(narrow - 1)]
    pairs += [(i * narrow + k + 1, i * narrow + k) for i in range(1, wide, 2) for k in range(narrow - 1)]
    halo = lax.ppermute(ordered(row_of(main), row_of(partner)), ("wide", "narrow"), pairs)

    def face(upper):
        index, holder = jnp.where(upper, size_x - 1, 0), jnp.where(upper, 1, 0)
        mine, other = (lax.dynamic_index_in_dim(x, index, 0, keepdims=False) for x in (basis, partner_raw))
        return jnp.where(core == holder, mine, other).reshape(size_y, depth)

    faces = [swap(face(chip % 2 == 0), "wide", 2)] if chips > 1 else []
    if chips > 2:
        ends = [(i, i + 2) for i in range(wide - 2) if i // 2 % 2 == 1]
        faces.append(lax.ppermute(face(chip % 2 == 1), "wide", ends + [(b, a) for a, b in ends]))

    turned_halo = swap(halo, "wide", 1)
    partner_kappa = swap(cell_kappa, "wide", 1)

    def rows_of(owner):
        return lax.dynamic_slice_in_dim(coefficients, owner * real, real, 0)

    def speed_of(owner):
        return 0.25 * lax.dynamic_slice_in_dim(velocity, owner * real, real, 1)

    def both(speed):
        return jnp.concatenate([speed, speed * jnp.array([[1.0], [1.0], [-1.0]], F32)], axis=1)

    state = jnp.concatenate([rows_of(w ^ (2 * j)) for j in range(chips)], axis=0)
    speed = both(jnp.concatenate([speed_of(w ^ (2 * j)) for j in range(chips)], axis=1))
    high = lax.reduce_precision(propagator, 8, 7)
    low = (propagator - high).astype(BF16)
    high = high.astype(BF16)
    place = jnp.stack([w, n]).astype(jnp.int32)

    def scratch(span, count):
        return [
            pltpu.VMEM((2 * count, depth), BF16),
            pltpu.VMEM((size_y + 2, span, 2 * count), F32),
            pltpu.VMEM((size_y, span, 2 * count), F32),
            pltpu.VMEM((size_y, span, 2 * count), BF16),
            pltpu.VMEM((2, size_y, 2 * count), F32),
        ]

    near = [main, partner, halo, turned_halo, cell_kappa, partner_kappa]
    passed = len(near)
    made = pl.pallas_call(
        functools.partial(first_kernel, dims, chips, real, passed),
        out_shape=[jax.ShapeDtypeStruct(x.shape, x.dtype) for x in near]
        + [jax.ShapeDtypeStruct((real, modes), F32)]
        + [jax.ShapeDtypeStruct((real, modes), BF16)] * (chips - 1),
        in_specs=[smem] + [vmem] * (passed + len(faces) + 2),
        out_specs=[vmem] * (passed + chips),
        scratch_shapes=scratch(2 * size_x, chips * real),
        input_output_aliases={i + 1: i for i in range(passed)},
        compiler_params=ROOM,
    )(place, *near, *faces, speed, state)
    near, total, sent = made[:passed], made[passed], made[passed + 1 :]
    got = [swap(x, "wide", 2 * (j + 1)) for j, x in enumerate(sent)]
    rest = jnp.concatenate(
        [near[0][half:], near[2], jnp.pad(near[4], ((0, 0), (0, depth - cells)))], axis=0
    )
    rests = [swap(rest, "wide", 2 * j) for j in range(1, chips)]
    far = []
    for j in range(1, chips):
        top, bottom = tops[j - 1], rests[j - 1]
        far += [top, bottom, swap(top, "wide", 1), swap(bottom, "wide", 1)]
    for x in got:
        total = total + x.astype(F32)

    def padded(x):
        return x if real == samples else jnp.pad(x, ((0, samples - real), (0, 0)))

    total = padded(total)
    sent = total.astype(BF16)
    others = [swap(sent, "narrow", d) for d in range(1, narrow)]
    speed = speed_of(w)
    speed = both(speed if real == samples else jnp.pad(speed, ((0, 0), (0, samples - real))))
    piece = (owned, modes)
    state, total, *sent = pl.pallas_call(
        functools.partial(next_kernel, dims, chips, narrow, factor, owned, passed),
        out_shape=[jax.ShapeDtypeStruct(piece, F32)] * 2 + [jax.ShapeDtypeStruct(piece, BF16)] * (narrow - 1),
        in_specs=[smem] + [vmem] * (passed + len(far) + 4 + narrow),
        out_specs=[vmem] * (narrow + 1),
        scratch_shapes=scratch(wide * size_x, samples) + [pltpu.VMEM((samples, modes), F32)] * 2,
        compiler_params=ROOM,
    )(place, *near, *far, speed, padded(rows_of(w)), high, low, total, *others)
    others = [swap(x, "narrow", d + 1) for d, x in enumerate(sent)]
    room = max(owned, 16)
    parts = [x if room == owned else jnp.pad(x, ((0, room - owned), (0, 0))) for x in (state, total, *others)]
    out = pl.pallas_call(
        functools.partial(last_kernel, factor),
        out_shape=jax.ShapeDtypeStruct((room, modes), F32),
        in_specs=[vmem] * (3 + narrow),
        out_specs=vmem,
        compiler_params=ROOM,
    )(parts[0], high, low, *parts[1:])
    return out[:owned]


def solution(mesh):
    placed = (
        P(("groups", "wide"), "narrow", None, None),
        P(("groups", "wide"), "narrow", None),
        P(None, "groups"),
        P("groups", None),
        P("groups", None),
    )

    return jax.shard_map(
        body,
        mesh=mesh,
        in_specs=placed,
        out_specs=P(("groups", "wide", "narrow"), None),
        check_vma=False,
    )
```
